256 devices in a mesh: grp: 8 (over y, core), dom: 32 (over x, z).
Axes of the slice: x: 4, y: 4, z: 8, core: 2. Of those that a mesh axis runs over, the one named last changes fastest.
Arguments:
- fine_nodes: bfloat16 [8, 24576, 128], P('grp', 'dom'), may hold values from -6 to 6
- fine_edges: bfloat16 [8, 294912, 128], P('grp', 'dom'), may hold values from -6 to 6
- fine_senders: int32 [8, 294912], P('grp', 'dom'), may hold values from 0 to 1535
- fine_receivers: int32 [8, 294912], P('grp', 'dom'), may hold values from 0 to 767, as said below
- edge_count: int32 [8, 32], P('grp', 'dom'), may hold values from 4608 to 9216, as said below
- ghost_send: int32 [8, 1024, 24], P('grp', 'dom'), may hold values from 0 to 767
- fine_parent: int32 [8, 24576], P('grp', 'dom'), may hold values from 0 to 16383, as said below
- coarse_nodes: bfloat16 [16384, 128], P('dom'), may hold values from -6 to 6
- coarse_edges: bfloat16 [131072, 128], P('dom'), may hold values from -6 to 6
- coarse_senders: int32 [131072], P('dom'), may hold values from 0 to 16383
- coarse_receivers: int32 [131072], P('dom'), may hold values from 0 to 511, as said below
- edge_in: bfloat16 [2, 384, 128], replicated, may hold values from -0.3125 to 0.3125
- node_in: bfloat16 [3, 256, 128], replicated, may hold values from -0.375 to 0.375
- mlp_out: bfloat16 [5, 128, 128], replicated, may hold values from -0.5 to 0.5
Outputs:
- fine_out: bfloat16 [8, 24576, 128], P('grp', 'dom')
- coarse_out: bfloat16 [16384, 128], P('dom')
The draws below stay inside these ranges and needn't reach their ends.
Inputs may be any that keep to these rules, and one draw needn't show every extreme that they name: `edge_count`: each device's live edge slot count; slots from that count on are padding; 9216 on at least one device. `fine_receivers`: nondecreasing along each device's 9216 slots; padding slots hold 767. `fine_senders`: below 768: a local node; 768 + s * 24 + k: ghost slot k received from dom index s of the same slab. `ghost_send`: local node indices; row p of a device's block lists the nodes sent to dom index p. `fine_parent`: global coarse index; owner o holds coarse nodes o * 512 to (o + 1) * 512 - 1. Most parents of a fine node of dom index d are owned by d itself; the others may be owned by any owner. `coarse_senders`: global coarse index of the sender. `coarse_receivers`: nondecreasing within each owner's 4096 edges.
All inputs are finite; a program needn't handle non-finite values.
Results may differ from the reference program's by a relative error of at most 0.015.
Values may be sent and summed in bfloat16 or wider, within the bound.
A program may use at most 64 MiB of HBM per device.

```python
import jax
import jax.numpy as jnp
from jax import lax

L = 128
NF_DEV = 768
C_DEV = 512
E_DEV = 9216
GH = 24
EC_DEV = 4096
COARSE = 16384
N_GRP = 8
N_DOM = 32


def ragged_edges(key):
    folded = jax.random.fold_in(key, 11)
    first, second, third = jax.random.split(folded, 3)
    counts = jax.random.randint(first, (N_GRP * N_DOM,), E_DEV // 2, E_DEV + 1)
    chosen = jax.random.randint(third, (), 0, N_GRP * N_DOM)
    counts = counts.at[chosen].set(E_DEV).astype(jnp.int32)
    base = jnp.sort(jax.random.randint(second, (N_GRP * N_DOM, E_DEV), 0, NF_DEV), axis=-1)
    slots = jnp.arange(E_DEV, dtype=jnp.int32)
    position = jnp.minimum(slots[None, :] * E_DEV // counts[:, None], E_DEV - 1)
    picked = jnp.take_along_axis(base, position, axis=-1)
    receivers = jnp.where(slots[None, :] < counts[:, None], picked, NF_DEV - 1)
    return (counts.reshape(N_GRP, N_DOM), receivers.reshape(N_GRP, N_DOM * E_DEV).astype(jnp.int32))


def draw_edge_count(key, part):
    return ragged_edges(key)[0]


def draw_fine_receivers(key, part):
    return ragged_edges(key)[1]


def draw_fine_parent(key, part):
    folded = jax.random.fold_in(key, 37)
    first, second, third = jax.random.split(folded, 3)
    shape = (N_GRP, N_DOM * NF_DEV)
    position = jnp.arange(N_DOM * NF_DEV, dtype=jnp.int32)
    domain = (position // NF_DEV)[None, :]
    spill = jax.random.randint(first, shape, 0, 100) < 25
    offset = jax.random.randint(second, shape, 1, N_DOM)
    offset = jnp.where(spill, offset, 0)
    offset = jnp.where((position % NF_DEV == 0)[None, :], N_DOM // 2, offset)
    owner = (domain + offset) % N_DOM
    within = jax.random.randint(third, shape, 0, C_DEV)
    return (owner * C_DEV + within).astype(jnp.int32)


def draw_coarse_receivers(key, part):
    folded = jax.random.fold_in(key, 23)
    raw = jax.random.randint(folded, (N_DOM, EC_DEV), 0, C_DEV)
    return jnp.sort(raw, axis=-1).reshape(N_DOM * EC_DEV).astype(jnp.int32)


def plant(values, own_key, smallest, largest):
    longest = values.shape.index(max(values.shape))
    spots = []
    for shift in (0, 1):
        where = [jax.random.randint(jax.random.fold_in(own_key, axis), (), 0, length) for axis, length in enumerate(values.shape)]
        where[longest] = (where[longest] + shift) % values.shape[longest]
        spots.append(tuple(where))
    return values.at[spots[0]].set(smallest).at[spots[1]].set(largest)


def block_scale(own_key, dims, pieces, low, largest):
    level = 1.0
    for axis_at, shards_of in pieces:
        draws = jax.random.uniform(jax.random.fold_in(jax.random.fold_in(own_key, 6), axis_at), (shards_of,), jnp.float32, low / len(pieces), largest / len(pieces))
        level = level * jnp.repeat(jnp.exp(draws), dims[axis_at] // shards_of).reshape((-1,) + (1,) * (len(dims) - 1 - axis_at))
    return level


def scatter_about(rng, shape, deviation, limit, cuts=(), kind=jnp.bfloat16):
    array = deviation * jax.random.normal(rng, shape, jnp.float32)
    if cuts:
        array = array * block_scale(rng, shape, cuts, -0.22, 0.18)
    return jnp.clip(array, -limit, limit).astype(kind)


def setup_inputs(seed: int = 0) -> dict:
    key_list = jax.random.split(jax.random.key(seed), 15)
    fine_nodes = scatter_about(key_list[0], (N_GRP, N_DOM * NF_DEV, L), 1.0, 6.0, ((0, 8), (1, 32)))
    fine_edges = scatter_about(key_list[1], (N_GRP, N_DOM * E_DEV, L), 1.0, 6.0, ((0, 8), (1, 32)))
    fine_senders = plant(jax.random.randint(key_list[2], (N_GRP, N_DOM * E_DEV), 0, NF_DEV + N_DOM * GH), jax.random.fold_in(key_list[2], 1), 0, (NF_DEV + N_DOM * GH) - 1).astype(jnp.int32)
    fine_receivers = draw_fine_receivers(jax.random.fold_in(key_list[14], 71), 0)
    edge_count = draw_edge_count(jax.random.fold_in(key_list[14], 71), 0)
    ghost_send = plant(jax.random.randint(key_list[5], (N_GRP, N_DOM * N_DOM, GH), 0, NF_DEV), jax.random.fold_in(key_list[5], 1), 0, NF_DEV - 1).astype(jnp.int32)
    fine_parent = draw_fine_parent(jax.random.fold_in(key_list[14], 71), 0)
    coarse_nodes = scatter_about(key_list[7], (COARSE, L), 1.0, 6.0, ((0, 32),))
    coarse_edges = scatter_about(key_list[8], (N_DOM * EC_DEV, L), 1.0, 6.0, ((0, 32),))
    coarse_senders = plant(jax.random.randint(key_list[9], (N_DOM * EC_DEV,), 0, COARSE), jax.random.fold_in(key_list[9], 1), 0, COARSE - 1).astype(jnp.int32)
    coarse_receivers = draw_coarse_receivers(jax.random.fold_in(key_list[14], 71), 0)
    edge_in = scatter_about(key_list[11], (2, 3 * L, L), (3 * L) ** -0.5, 0.3125)
    node_in = scatter_about(key_list[12], (3, 2 * L, L), (2 * L) ** -0.5, 0.375)
    mlp_out = scatter_about(key_list[13], (5, L, L), L ** -0.5, 0.5)
    return dict(fine_nodes=fine_nodes, fine_edges=fine_edges, fine_senders=fine_senders, fine_receivers=fine_receivers, edge_count=edge_count, ghost_send=ghost_send, fine_parent=fine_parent, coarse_nodes=coarse_nodes, coarse_edges=coarse_edges, coarse_senders=coarse_senders, coarse_receivers=coarse_receivers, edge_in=edge_in, node_in=node_in, mlp_out=mlp_out)


def layer_norm(values):
    centre = values - lax.optimization_barrier(jnp.mean(values, -1, keepdims=True))
    spread = lax.optimization_barrier(jnp.mean(centre * centre, -1, keepdims=True))
    return centre * lax.rsqrt(spread + 1e-05)

def perceptron(inputs, w_first, w_second):
    hidden = jax.nn.silu(jnp.dot(inputs, w_first, preferred_element_type=jnp.float32)).astype(jnp.bfloat16)
    return layer_norm(jnp.dot(hidden, w_second, preferred_element_type=jnp.float32))

def reference(fine_nodes, fine_edges, fine_senders, fine_receivers, edge_count, ghost_send, fine_parent, coarse_nodes, coarse_edges, coarse_senders, coarse_receivers, edge_in, node_in, mlp_out):
    devices_all = N_GRP * N_DOM
    nodes_all = fine_nodes.reshape(N_GRP, N_DOM, NF_DEV, L)
    edges_all = fine_edges.reshape(devices_all, E_DEV, L)
    senders_all = fine_senders.reshape(devices_all, E_DEV)
    receivers_all = fine_receivers.reshape(devices_all, E_DEV)
    counts_all = edge_count.reshape(devices_all)
    sends_all = ghost_send.reshape(N_GRP, N_DOM, N_DOM, GH)
    parents_all = fine_parent.reshape(devices_all, NF_DEV)
    peers = jnp.arange(N_DOM)

    def fine_step(index):
        group = index // N_DOM
        domain = index % N_DOM
        local = nodes_all[group, domain]
        picks = sends_all[group, :, domain, :]
        ghosts = nodes_all[group][peers[:, None], picks]
        table = jnp.concatenate([local, ghosts.reshape(N_DOM * GH, L)], 0)
        edges = edges_all[index]
        receivers = receivers_all[index]
        inputs = jnp.concatenate([edges, local[receivers], table[senders_all[index]]], -1)
        edge_new = edges.astype(jnp.float32) + perceptron(inputs, edge_in[0], mlp_out[0])
        live = (jnp.arange(E_DEV) < counts_all[index]).astype(jnp.float32)
        summed = jax.ops.segment_sum(edge_new * live[:, None], receivers, num_segments=NF_DEV).astype(jnp.bfloat16)
        node_new = local.astype(jnp.float32) + perceptron(jnp.concatenate([local, summed], -1), node_in[0], mlp_out[1])
        return node_new.astype(jnp.bfloat16)
    fine_mid = lax.map(fine_step, jnp.arange(devices_all))
    flat_parent = parents_all.reshape(-1)
    pooled = jax.ops.segment_sum(fine_mid.reshape(-1, L).astype(jnp.float32), flat_parent, num_segments=COARSE)
    children = jax.ops.segment_sum(jnp.ones(flat_parent.shape, jnp.float32), flat_parent, num_segments=COARSE)
    coarse_mid = ((coarse_nodes.astype(jnp.float32) + pooled) / (1.0 + children)[:, None]).astype(jnp.bfloat16)
    cedges_all = coarse_edges.reshape(N_DOM, EC_DEV, L)
    csend_all = coarse_senders.reshape(N_DOM, EC_DEV)
    crecv_all = coarse_receivers.reshape(N_DOM, EC_DEV)
    cmid_all = coarse_mid.reshape(N_DOM, C_DEV, L)

    def coarse_step(owner):
        own = cmid_all[owner]
        cedges = cedges_all[owner]
        receivers = crecv_all[owner]
        inputs = jnp.concatenate([cedges, own[receivers], coarse_mid[csend_all[owner]]], -1)
        cedge_new = cedges.astype(jnp.float32) + perceptron(inputs, edge_in[1], mlp_out[2])
        summed = jax.ops.segment_sum(cedge_new, receivers, num_segments=C_DEV).astype(jnp.bfloat16)
        updated = own.astype(jnp.float32) + perceptron(jnp.concatenate([own, summed], -1), node_in[1], mlp_out[3])
        return updated.astype(jnp.bfloat16)
    coarse_out = lax.map(coarse_step, jnp.arange(N_DOM)).reshape(COARSE, L)

    def return_step(index):
        middle = fine_mid[index]
        above = coarse_out[parents_all[index]]
        updated = middle.astype(jnp.float32) + perceptron(jnp.concatenate([middle, above], -1), node_in[2], mlp_out[4])
        return updated.astype(jnp.bfloat16)
    fine_out = lax.map(return_step, jnp.arange(devices_all)).reshape(N_GRP, N_DOM * NF_DEV, L)
    return (fine_out, coarse_out)
```

```python
import functools

import jax
import jax.numpy as jnp
from jax import lax
from jax.experimental import pallas as pl
from jax.experimental.pallas import tpu as pltpu
from jax.sharding import PartitionSpec as P

BF = jnp.bfloat16
F32 = jnp.float32
I32 = jnp.int32
POOL = 24
POOL_PAD = 32
ASK = 48
ASK_PAD = 64
NT = (((1,), (1,)), ((), ()))


def dot(a, b):
    return jnp.dot(a, b, preferred_element_type=F32)


def iota(shape, axis):
    return lax.broadcasted_iota(I32, shape, axis)


def as_bf(mask):
    return jnp.where(mask, 1.0, 0.0).astype(BF)


def column(row):
    n = row.shape[1]
    return jnp.concatenate(
        [jnp.broadcast_to(row[:, k : k + 128], (128, 128)).T for k in range(0, n, 128)], 0
    )


def pick_rows(col, width):
    n = col.shape[0]
    lane = iota((n, 128), 1)
    return jnp.concatenate([as_bf(col == lane + k) for k in range(0, width, 128)], 1)


def pick_into(row, height, first=0):
    return as_bf(iota((height, row.shape[1]), 0) + first == row)


def mean_of(w):
    mean = jnp.mean(w.astype(F32), axis=1, keepdims=True)
    return jnp.concatenate([w, jnp.broadcast_to(mean, w.shape).astype(BF)], axis=1)


def averager():
    return jnp.full((128, 128), 1.0 / 128, BF)


def second(x, w_mean, ones):
    hidden = (x / (1.0 + jnp.exp(-x))).astype(BF)
    y = dot(hidden, w_mean)
    centre = y[:, :128] - y[:, 128:]
    spread = dot((centre * centre).astype(BF), ones)
    return centre * lax.rsqrt(spread + 1e-5)


def vmem(n):
    return [pl.BlockSpec(memory_space=pltpu.VMEM)] * n


def fine_kernel(
    block, count, edges_ref, snd_ref, rcv_ref, local_ref, ghost_ref, ein_ref, nin_ref, out_w, out_ref,
    by_sender, by_receiver, total, w_mean,
):
    step = pl.program_id(0)
    nodes = local_ref.shape[0]
    half = nodes // 2
    ones = averager()

    @pl.when(step == 0)
    def _():
        local = local_ref[...]
        by_sender[:, :128] = dot(local, ein_ref[0, 256:384, :]).astype(BF)
        by_sender[:, 128:] = dot(ghost_ref[...], ein_ref[0, 256:384, :]).astype(BF)
        mine = dot(local, ein_ref[0, 128:256, :]).astype(BF)
        by_receiver[:, :128] = mine[:half]
        by_receiver[:, 128:] = mine[half:]
        total[...] = jnp.zeros_like(total)
        w_mean[0] = mean_of(out_w[0])
        w_mean[1] = mean_of(out_w[1])

    receivers = rcv_ref[0]
    scol = column(snd_ref[0])
    rcol = column(receivers)
    s_upper = scol >= nodes
    r_upper = rcol >= half
    from_s = dot(pick_rows(jnp.where(s_upper, scol - nodes, scol), nodes), by_sender[...])
    from_r = dot(pick_rows(jnp.where(r_upper, rcol - half, rcol), half), by_receiver[...])
    edge = edges_ref[...]
    x = (
        dot(edge, ein_ref[0, 0:128, :])
        + jnp.where(s_upper, from_s[:, 128:], from_s[:, :128])
        + jnp.where(r_upper, from_r[:, 128:], from_r[:, :128])
    )
    new = edge.astype(F32) + second(x, w_mean[0], ones)
    sides = jnp.concatenate([jnp.where(r_upper, 0.0, new), jnp.where(r_upper, new, 0.0)], 1)
    slot = step * block + iota((1, block), 1)
    into = jnp.where(receivers >= half, receivers - half, receivers)
    into = jnp.where(slot < count[0, 0], into, -1)
    total[...] += dot(pick_into(into, half), sides.astype(BF))

    @pl.when(step == pl.num_programs(0) - 1)
    def _():
        agg = jnp.concatenate([total[:, :128], total[:, 128:]], 0).astype(BF)
        local = local_ref[...]
        x = dot(local, nin_ref[0, 0:128, :]) + dot(agg, nin_ref[0, 128:256, :])
        out_ref[...] = (local.astype(F32) + second(x, w_mean[1], ones)).astype(BF)


def fine_step(count, edges, senders, receivers, local, ghost, edge_in, node_in, mlp_out, block=1024):
    slots, nodes = edges.shape[0], local.shape[0]
    steps = slots // block
    whole = lambda a: pl.BlockSpec(a.shape, lambda i: (0,) * a.ndim)
    index = pl.BlockSpec((1, 1, block), lambda i: (i, 0, 0))
    return pl.pallas_call(
        functools.partial(fine_kernel, block),
        grid=(steps,),
        name="fine_edges",
        out_shape=jax.ShapeDtypeStruct((nodes, 128), BF),
        in_specs=[
            pl.BlockSpec(memory_space=pltpu.SMEM), pl.BlockSpec((block, 128), lambda i: (i, 0)), index, index,
            whole(local), whole(ghost), whole(edge_in), whole(node_in), whole(mlp_out),
        ],
        out_specs=pl.BlockSpec((nodes, 128), lambda i: (0, 0)),
        scratch_shapes=[
            pltpu.VMEM((nodes, 256), BF), pltpu.VMEM((nodes // 2, 256), BF), pltpu.VMEM((nodes // 2, 256), F32),
            pltpu.VMEM((2, 128, 256), BF),
        ],
    )(
        count, edges, senders.reshape(steps, 1, block), receivers.reshape(steps, 1, block),
        local, ghost, edge_in, node_in, mlp_out,
    )


def each_peer(axis, body):
    me, peers = lax.axis_index(axis), lax.axis_size(axis)

    def one(step, carry):
        body(lax.rem(me + step, peers))
        return carry

    lax.fori_loop(1, peers, one, 0)


def greet(axes):
    barrier = pltpu.get_barrier_semaphore()
    for axis in axes:
        each_peer(axis, lambda peer, axis=axis: pl.semaphore_signal(barrier, inc=1, device_id={axis: peer}))


def all_here(axes):
    pl.semaphore_wait(pltpu.get_barrier_semaphore(), sum(lax.axis_size(axis) - 1 for axis in axes))


def send(axis, source, target, sems):
    me = lax.axis_index(axis)

    def one(peer):
        pltpu.make_async_remote_copy(
            src_ref=source(peer), dst_ref=target(me), send_sem=sems.at[0], recv_sem=sems.at[1],
            device_id={axis: peer},
        ).start()

    each_peer(axis, one)


def arrived(axis, span, sems):
    peer = lax.rem(lax.axis_index(axis) + 1, lax.axis_size(axis))
    whole = pltpu.make_async_remote_copy(
        src_ref=span, dst_ref=span, send_sem=sems.at[0], recv_sem=sems.at[1], device_id={axis: peer}
    )
    whole.wait()


def ranked(owner, owners):
    n = owner.shape[1]
    theirs = iota((owners, n), 0) == owner
    before = as_bf(iota((n, n), 0) < iota((n, n), 1))
    counts = dot(as_bf(theirs), before)
    return jnp.sum(jnp.where(theirs, counts, 0.0), axis=0, keepdims=True).astype(I32), theirs


def listed(theirs, value, lane):
    n = value.shape[1]
    code = value + 1
    low, high = (code & 255).astype(F32), (code >> 8).astype(F32)
    parts = jnp.concatenate([jnp.where(theirs, low, 0.0), jnp.where(theirs, high, 0.0)], 0)
    there = as_bf(iota((128, n), 0) == lane)
    out = lax.dot_general(parts.astype(BF), there, NT, preferred_element_type=F32)
    owners = theirs.shape[0]
    return (out[:owners] + 256.0 * out[owners:]).astype(I32)


def early_kernel(
    local_ref, ghost_ids, parents, csenders, ghost_out, place_out, cplace_out, pool_out, ask_out, flag_out,
    ghost_tx, ghost_rx, note_tx, note_rx, flag_rx, flag_tx, ghost_sems, note_sems, flag_sems,
):
    me, grp = lax.axis_index("dom"), lax.axis_index("grp")
    peers, groups = lax.axis_size("dom"), lax.axis_size("grp")
    shift = 9
    rows = ghost_tx.shape[1]
    greet(("dom", "grp"))
    picks = dot(pick_rows(column(ghost_ids[...]), local_ref.shape[0]), local_ref[...])
    for p in range(peers):
        ghost_tx[p] = picks[p * rows : (p + 1) * rows].astype(BF)

    all_here(("dom", "grp"))
    send("dom", lambda peer: ghost_tx.at[peer], lambda me: ghost_rx.at[me], ghost_sems)
    ghost_rx[me] = ghost_tx[me]

    parent = parents[...]
    owner, within = parent >> shift, parent & ((1 << shift) - 1)
    rank, theirs = ranked(owner, peers)
    away = owner != me
    place_out[...] = jnp.where(away, (1 << shift) + owner * POOL_PAD + rank, within)
    excess = jnp.max(jnp.where(away & (rank >= POOL), 1, 0), axis=1, keepdims=True)
    pool_note = listed(theirs, within, rank + lax.rem(me, 4) * POOL_PAD)

    sender = csenders[grp]
    owner, within = sender >> shift, sender & ((1 << shift) - 1)
    rank, theirs = ranked(owner, peers)
    away = owner != me
    cplace_out[...] = jnp.where(away, (1 << shift) + owner * ASK_PAD + rank, within)
    excess = jnp.maximum(excess, jnp.max(jnp.where(away & (rank >= ASK), 1, 0), axis=1, keepdims=True))
    ask_note = listed(theirs, within, rank + lax.rem(me, 2) * ASK_PAD)

    flag_tx[...] = jnp.broadcast_to(excess, (1, 128))
    send("grp", lambda peer: flag_tx, lambda grp: flag_rx.at[grp], flag_sems)
    flag_rx[grp] = flag_tx[...]
    for p in range(peers):
        note_tx[p, :, 0:128] = pool_note[p : p + 1]
        note_tx[p, :, 128:256] = ask_note[p : p + 1]
    arrived("grp", flag_rx.at[pl.ds(0, groups - 1)], flag_sems)
    flag = flag_rx[0]
    for k in range(1, groups):
        flag = jnp.maximum(flag, flag_rx[k])
    for p in range(peers):
        note_tx[p, :, 256:384] = flag
    send("dom", lambda peer: note_tx.at[peer], lambda me: note_rx.at[me], note_sems)
    note_rx[me] = jnp.concatenate([jnp.zeros((1, 256), I32), flag], 1)
    arrived("dom", note_rx.at[pl.ds(0, peers - 1)], note_sems)
    notes = [note_rx[p] for p in range(peers)]
    for k in range(0, peers, 4):
        pool_out[k // 4 : k // 4 + 1, :] = sum(n[:, 0:128] for n in notes[k : k + 4])
    for k in range(0, peers, 2):
        ask_out[k // 2 : k // 2 + 1, :] = sum(n[:, 128:256] for n in notes[k : k + 2])
    for n in notes:
        flag = jnp.maximum(flag, n[:, 256:384])
    flag_out[...] = flag
    arrived("dom", ghost_rx.at[pl.ds(0, peers - 1)], ghost_sems)
    ghost_out[...] = ghost_rx[...]


def early_step(local, ghost_send, parents, csenders, groups):
    peers, rows = ghost_send.shape
    edges = csenders.shape[0] // groups
    return pl.pallas_call(
        early_kernel,
        name="early",
        out_shape=[
            jax.ShapeDtypeStruct((peers, rows, 128), BF),
            jax.ShapeDtypeStruct((1, parents.shape[0]), I32),
            jax.ShapeDtypeStruct((1, edges), I32),
            jax.ShapeDtypeStruct((peers // 4, 128), I32),
            jax.ShapeDtypeStruct((peers // 2, 128), I32),
            jax.ShapeDtypeStruct((1, 128), I32),
        ],
        in_specs=vmem(4),
        out_specs=vmem(6),
        scratch_shapes=[
            pltpu.VMEM((peers, rows, 128), BF), pltpu.VMEM((peers, rows, 128), BF),
            pltpu.VMEM((peers, 1, 384), I32), pltpu.VMEM((peers, 1, 384), I32),
            pltpu.VMEM((groups, 1, 128), I32), pltpu.VMEM((1, 128), I32),
            pltpu.SemaphoreType.DMA((2,)), pltpu.SemaphoreType.DMA((2,)), pltpu.SemaphoreType.DMA((2,)),
        ],
        compiler_params=pltpu.CompilerParams(collective_id=0, has_side_effects=True),
    )(local, ghost_send.reshape(1, -1), parents.reshape(1, -1), csenders.reshape(groups, 1, edges))


def late_kernel(
    mid_ref, place_ref, cplace_ref, pool_ref, ask_ref, cnodes_ref, cedges_hbm, crecv_ref, ein_ref, nin_ref, out_w,
    fine_out, coarse_out,
    cedges, up_tx, up_rx, count_tx, count_rx, part_tx, part_rx, cmid, ask_tx, ask_rx, cpart_tx, cpart_rx, cout,
    down_tx, down_rx, ask_sel, down_sel, csel, fsel, edge_sem, sems,
):
    me, grp = lax.axis_index("dom"), lax.axis_index("grp")
    peers, groups = lax.axis_size("dom"), lax.axis_size("grp")
    others, friends = peers - 1, groups - 1
    own = cnodes_ref.shape[0]
    piece = own // groups
    nedges = cedges.shape[0]
    ones = averager()
    ups, asks = peers * POOL_PAD, peers * ASK_PAD
    fetch = pltpu.make_async_copy(
        cedges_hbm.at[pl.ds(pl.multiple_of(grp * nedges, nedges), nedges)], cedges, edge_sem
    )
    fetch.start()
    up_rx[...] = jnp.zeros_like(up_rx)
    down_rx[...] = jnp.zeros_like(down_rx)
    ask_rx[...] = jnp.zeros_like(ask_rx)
    greet(("dom", "grp"))

    mid, place = mid_ref[...], place_ref[...]
    up_tx[...] = dot(pick_into(place, ups, own), mid).astype(BF).reshape(up_tx.shape)
    all_here(("dom", "grp"))
    few, some = pl.ds(0, POOL), pl.ds(0, ASK)
    send("dom", lambda p: up_tx.at[p, few], lambda m: up_rx.at[m, few], sems.at[0])

    here = pick_into(place, own)
    pool_rows = jnp.concatenate([pool_ref[k : k + 1, :] for k in range(pool_ref.shape[0])], 1) - 1
    there = pick_into(pool_rows, own)
    counts = lax.dot_general(jnp.full((8, here.shape[1]), 1.0, BF), here, NT, preferred_element_type=F32)
    counts += lax.dot_general(jnp.full((8, ups), 1.0, BF), there, NT, preferred_element_type=F32)
    count_tx[...] = counts[0:1]
    send("grp", lambda p: count_tx, lambda m: count_rx.at[m], sems.at[1])
    count_rx[grp] = count_tx[...]
    pooled = dot(here, mid)
    for k in range(ask_ref.shape[0]):
        ask_sel[128 * k : 128 * (k + 1), :] = pick_rows(column(ask_ref[k : k + 1, :] - 1), own)
    for k in range(pool_ref.shape[0]):
        down_sel[128 * k : 128 * (k + 1), :] = pick_rows(column(pool_ref[k : k + 1, :] - 1), own)
    csel[...] = pick_rows(column(cplace_ref[...]), own + asks)
    fsel[...] = pick_rows(column(place), own + ups)
    receivers = crecv_ref[grp]
    into = pick_into(receivers, own)
    from_r = pick_rows(column(receivers), own)
    w_edge, w_node, w_back = mean_of(out_w[2]), mean_of(out_w[3]), mean_of(out_w[4])
    arrived("grp", count_rx.at[pl.ds(0, friends)], sems.at[1])
    children = count_rx[0]
    for k in range(1, groups):
        children = children + count_rx[k]
    diagonal = iota((piece, own), 1) == iota((piece, own), 0) + grp * piece
    children = jnp.sum(jnp.where(diagonal, children, 0.0), axis=1, keepdims=True)

    arrived("dom", up_rx.at[pl.ds(0, others), few], sems.at[0])
    pooled += dot(there, up_rx[...].reshape(ups, 128))
    part_tx[...] = pooled.astype(BF).reshape(part_tx.shape)
    send("grp", lambda p: part_tx.at[p], lambda m: part_rx.at[m], sems.at[2])
    part_rx[grp] = part_tx[grp]
    arrived("grp", part_rx.at[pl.ds(0, friends)], sems.at[2])
    mine = pl.ds(pl.multiple_of(grp * piece, piece), piece)
    sums = cnodes_ref[mine, :].astype(F32)
    for k in range(groups):
        sums = sums + part_rx[k].astype(F32)
    own_mid = (sums / (1.0 + children)).astype(BF)
    cmid[grp] = own_mid
    send("grp", lambda p: cmid.at[grp], lambda m: cmid.at[m], sems.at[3])
    arrived("grp", cmid.at[pl.ds(0, friends)], sems.at[3])

    coarse = cmid[...].reshape(own, 128)
    ask_tx[...] = dot(ask_sel[...], coarse).astype(BF).reshape(ask_tx.shape)
    send("dom", lambda p: ask_tx.at[p, some], lambda m: ask_rx.at[m, some], sems.at[4])
    fetch.wait()
    edge = cedges[...]
    x = dot(edge, ein_ref[1, 0:128, :]) + dot(dot(from_r, coarse).astype(BF), ein_ref[1, 128:256, :])
    sender = dot(csel[:, 0:own], coarse)
    arrived("dom", ask_rx.at[pl.ds(0, others), some], sems.at[4])
    sender += dot(csel[:, own:], ask_rx[...].reshape(asks, 128))
    x += dot(sender.astype(BF), ein_ref[1, 256:384, :])
    new = edge.astype(F32) + second(x, w_edge, ones)
    cpart_tx[...] = dot(into, new.astype(BF)).astype(BF).reshape(cpart_tx.shape)
    send("grp", lambda p: cpart_tx.at[p], lambda m: cpart_rx.at[m], sems.at[5])
    cpart_rx[grp] = cpart_tx[grp]
    x = dot(own_mid, nin_ref[1, 0:128, :])
    arrived("grp", cpart_rx.at[pl.ds(0, friends)], sems.at[5])
    sums = cpart_rx[0].astype(F32)
    for k in range(1, groups):
        sums = sums + cpart_rx[k].astype(F32)
    x += dot(sums.astype(BF), nin_ref[1, 128:256, :])
    cout[grp] = (own_mid.astype(F32) + second(x, w_node, ones)).astype(BF)
    send("grp", lambda p: cout.at[grp], lambda m: cout.at[m], sems.at[6])
    arrived("grp", cout.at[pl.ds(0, friends)], sems.at[6])

    coarse = cout[...].reshape(own, 128)
    down_tx[...] = dot(down_sel[...], coarse).astype(BF).reshape(down_tx.shape)
    send("dom", lambda p: down_tx.at[p, few], lambda m: down_rx.at[m, few], sems.at[7])
    coarse_out[...] = coarse
    above = dot(fsel[:, 0:own], coarse)
    x = dot(mid, nin_ref[2, 0:128, :])
    arrived("dom", down_rx.at[pl.ds(0, others), few], sems.at[7])
    above += dot(fsel[:, own:], down_rx[...].reshape(ups, 128))
    x += dot(above.astype(BF), nin_ref[2, 128:256, :])
    fine_out[...] = (mid.astype(F32) + second(x, w_back, ones)).astype(BF)


def late_step(
    mid, place, cplace, pool, ask, coarse_nodes, coarse_edges, coarse_receivers, edge_in, node_in, mlp_out
):
    peers, groups = lax.axis_size("dom"), lax.axis_size("grp")
    own, nodes = coarse_nodes.shape[0], mid.shape[0]
    edges, piece = coarse_edges.shape[0] // groups, own // groups
    pieces = lambda: pltpu.VMEM((groups, piece, 128), BF)
    specs = vmem(6) + [pl.BlockSpec(memory_space=pl.ANY)] + vmem(4)
    return pl.pallas_call(
        late_kernel,
        name="late",
        out_shape=[jax.ShapeDtypeStruct((nodes, 128), BF), jax.ShapeDtypeStruct((own, 128), BF)],
        in_specs=specs,
        out_specs=vmem(2),
        scratch_shapes=[
            pltpu.VMEM((edges, 128), BF),
            pltpu.VMEM((peers, POOL_PAD, 128), BF), pltpu.VMEM((peers, POOL_PAD, 128), BF),
            pltpu.VMEM((1, own), F32), pltpu.VMEM((groups, 1, own), F32),
            pieces(), pieces(), pieces(),
            pltpu.VMEM((peers, ASK_PAD, 128), BF), pltpu.VMEM((peers, ASK_PAD, 128), BF),
            pieces(), pieces(), pieces(),
            pltpu.VMEM((peers, POOL_PAD, 128), BF), pltpu.VMEM((peers, POOL_PAD, 128), BF),
            pltpu.VMEM((peers * ASK_PAD, own), BF), pltpu.VMEM((peers * POOL_PAD, own), BF),
            pltpu.VMEM((edges, own + peers * ASK_PAD), BF), pltpu.VMEM((nodes, own + peers * POOL_PAD), BF),
            pltpu.SemaphoreType.DMA, pltpu.SemaphoreType.DMA((8, 2)),
        ],
        compiler_params=pltpu.CompilerParams(collective_id=1, has_side_effects=True),
    )(
        mid, place, cplace, pool, ask, coarse_nodes, coarse_edges, coarse_receivers.reshape(groups, 1, edges),
        edge_in, node_in, mlp_out,
    )


def layer_norm(values):
    centre = values - jnp.mean(values, -1, keepdims=True)
    spread = jnp.mean(centre * centre, -1, keepdims=True)
    return centre * lax.rsqrt(spread + 1e-05)


def perceptron(inputs, w_first, w_second):
    hidden = jax.nn.silu(jnp.dot(inputs, w_first, preferred_element_type=F32)).astype(BF)
    return layer_norm(jnp.dot(hidden, w_second, preferred_element_type=F32))


def summed(array, axis):
    return jnp.sum(lax.all_to_all(array, axis, 0, 0, tiled=True), axis=0)


def all_of(array, axis):
    peers = lax.axis_size(axis)
    copies = lax.all_to_all(jnp.broadcast_to(array[None], (peers, *array.shape)), axis, 0, 0, tiled=True)
    return copies.reshape(peers * array.shape[0], *array.shape[1:])


def dense_step(
    mid, parents, coarse_nodes, coarse_edges, coarse_senders, coarse_receivers, edge_in, node_in, mlp_out
):
    peers, groups = lax.axis_size("dom"), lax.axis_size("grp")
    own = coarse_nodes.shape[0]
    piece = own // groups
    wide = jnp.concatenate([mid.astype(F32), jnp.ones(mid.shape, F32)], -1)
    sums = jax.ops.segment_sum(wide, parents, num_segments=own * peers)
    sums = jnp.moveaxis(sums.reshape(peers, groups, piece, 256), 1, 0)
    sums = all_of(summed(summed(sums, "grp"), "dom"), "grp")
    coarse_mid = ((coarse_nodes.astype(F32) + sums[:, :128]) / (1.0 + sums[:, 128:])).astype(BF)
    table = all_of(coarse_mid, "dom")
    inputs = jnp.concatenate([coarse_edges, coarse_mid[coarse_receivers], table[coarse_senders]], -1)
    new = coarse_edges.astype(F32) + perceptron(inputs, edge_in[1], mlp_out[2])
    agg = jax.ops.segment_sum(new, coarse_receivers, num_segments=own).astype(BF)
    out = perceptron(jnp.concatenate([coarse_mid, agg], -1), node_in[1], mlp_out[3])
    coarse_out = (coarse_mid.astype(F32) + out).astype(BF)
    above = all_of(coarse_out, "dom")[parents]
    back = perceptron(jnp.concatenate([mid, above], -1), node_in[2], mlp_out[4])
    return (mid.astype(F32) + back).astype(BF), coarse_out


def per_device(
    fine_nodes, fine_edges, fine_senders, fine_receivers, edge_count, ghost_send, fine_parent, coarse_nodes,
    coarse_edges, coarse_senders, coarse_receivers, edge_in, node_in, mlp_out,
):
    groups = lax.axis_size("grp")
    local, parents = fine_nodes[0], fine_parent[0]
    ghosts, place, cplace, pool, ask, flag = early_step(local, ghost_send[0], parents, coarse_senders, groups)
    mid = fine_step(
        edge_count, fine_edges[0], fine_senders[0], fine_receivers[0], local, ghosts.reshape(-1, 128),
        edge_in, node_in, mlp_out,
    )

    def listed_step():
        return late_step(
            mid, place, cplace, pool, ask, coarse_nodes, coarse_edges, coarse_receivers, edge_in, node_in, mlp_out
        )

    def whole_step():
        return dense_step(
            mid, parents, coarse_nodes, coarse_edges, coarse_senders, coarse_receivers, edge_in, node_in, mlp_out
        )

    fine_out, coarse_out = lax.cond(flag[0, 0] > 0, whole_step, listed_step)
    return (fine_out[None], coarse_out)


def solution(mesh):
    fine, coarse = P("grp", "dom"), P("dom")
    in_specs = (fine,) * 7 + (coarse,) * 4 + (P(),) * 3
    return jax.shard_map(
        per_device, mesh=mesh, in_specs=in_specs, out_specs=(fine, coarse), check_vma=False
    )
```

```python
import functools

import jax
import jax.numpy as jnp
from jax import lax
from jax.experimental import pallas as pl
from jax.experimental.pallas import tpu as pltpu
from jax.sharding import PartitionSpec as P

BF = jnp.bfloat16
F32 = jnp.float32
I32 = jnp.int32
POOL = 24
POOL_PAD = 32
ASK = 24
AXIS_SHAPE = {"dom": (4, 8), "grp": (4, 2)}
BLOCK = 1024
EARLY_BLOCKS = 4
NT = (((1,), (1,)), ((), ()))


def dot(a, b):
    return jnp.dot(a, b, preferred_element_type=F32)


def iota(shape, axis):
    return lax.broadcasted_iota(I32, shape, axis)


def as_bf(mask):
    return jnp.where(mask, 1.0, 0.0).astype(BF)


def column(row):
    n = row.shape[1]
    return jnp.concatenate(
        [jnp.broadcast_to(row[:, k : k + 128], (128, 128)).T for k in range(0, n, 128)], 0
    )


def pick_rows(col, width):
    n = col.shape[0]
    lane = iota((n, 128), 1)
    return jnp.concatenate([as_bf(col == lane + k) for k in range(0, width, 128)], 1)


def pick_into(row, height, first=0):
    return as_bf(iota((height, row.shape[1]), 0) + first == row)


def mean_of(w):
    mean = jnp.mean(w.astype(F32), axis=1, keepdims=True)
    return jnp.concatenate([w, jnp.broadcast_to(mean, w.shape).astype(BF)], axis=1)


def averager():
    return jnp.full((128, 128), 1.0 / 128, BF)


def second(x, w_mean, ones):
    hidden = (x / (1.0 + jnp.exp(-x))).astype(BF)
    y = dot(hidden, w_mean)
    centre = y[:, :128] - y[:, 128:]
    spread = dot((centre * centre).astype(BF), ones)
    return centre * lax.rsqrt(spread + 1e-5)


def vmem(n):
    return [pl.BlockSpec(memory_space=pltpu.VMEM)] * n


def each_peer(axis, body):
    rows, columns = AXIS_SHAPE[axis]
    me = lax.axis_index(axis)
    row, column_ = me // columns, lax.rem(me, columns)
    wrapped = lambda d, n: min(d, n - d)
    steps = [(r, c) for r in range(rows) for c in range(columns) if r or c]
    steps.sort(key=lambda s: -wrapped(s[0], rows) - wrapped(s[1], columns))
    for r, c in steps:
        body(lax.rem(row + r, rows) * columns + lax.rem(column_ + c, columns))


def greet(axes):
    barrier = pltpu.get_barrier_semaphore()
    for axis in axes:
        each_peer(axis, lambda peer, axis=axis: pl.semaphore_signal(barrier, inc=1, device_id={axis: peer}))


def all_here(axes):
    pl.semaphore_wait(pltpu.get_barrier_semaphore(), sum(lax.axis_size(axis) - 1 for axis in axes))


def send(axis, source, target, sems):
    me = lax.axis_index(axis)

    def one(peer):
        pltpu.make_async_remote_copy(
            src_ref=source(peer), dst_ref=target(me), send_sem=sems.at[0], recv_sem=sems.at[1],
            device_id={axis: peer},
        ).start()

    each_peer(axis, one)


def arrived(axis, span, sems):
    peer = lax.rem(lax.axis_index(axis) + 1, lax.axis_size(axis))
    whole = pltpu.make_async_remote_copy(
        src_ref=span, dst_ref=span, send_sem=sems.at[0], recv_sem=sems.at[1], device_id={axis: peer}
    )
    whole.wait()


def ranked(owner, owners):
    n = owner.shape[1]
    theirs = iota((owners, n), 0) == owner
    before = as_bf(iota((n, n), 0) < iota((n, n), 1))
    counts = dot(as_bf(theirs), before)
    return jnp.sum(jnp.where(theirs, counts, 0.0), axis=0, keepdims=True).astype(I32), theirs


def listed(theirs, value, lane):
    n = value.shape[1]
    code = value + 1
    low, high = (code & 255).astype(F32), (code >> 8).astype(F32)
    parts = jnp.concatenate([jnp.where(theirs, low, 0.0), jnp.where(theirs, high, 0.0)], 0)
    there = as_bf(iota((128, n), 0) == lane)
    out = lax.dot_general(parts.astype(BF), there, NT, preferred_element_type=F32)
    owners = theirs.shape[0]
    return (out[:owners] + 256.0 * out[owners:]).astype(I32)


def step_kernel(
    count_ref, edges_hbm, snd_ref, rcv_ref, local_ref, ghost_ids, parents, csenders, cnodes_ref, cedges_hbm,
    crecv_ref, ein_ref, nin_ref, out_w,
    fine_out, coarse_out, mid_out, flag_out,
    edges, partial, by_sender, by_receiver, total, w_mean, cedges,
    ghost_tx, ghost_rx, note_tx, note_rx, flag_tx, flag_rx,
    up_tx, up_rx, count_tx, count_rx, part_tx, part_rx, cmid, ask_tx, ask_rx, cpart_tx, cpart_rx, cout,
    down_tx, down_rx, ask_sel, down_sel, fsel, cedge, cto, fetch_sems, sems,
):
    me, grp = lax.axis_index("dom"), lax.axis_index("grp")
    peers, groups = lax.axis_size("dom"), lax.axis_size("grp")
    others, friends = peers - 1, groups - 1
    nodes = local_ref.shape[0]
    half = nodes // 2
    blocks, _, block = snd_ref.shape
    own = cnodes_ref.shape[0]
    shift = own.bit_length() - 1
    piece = own // groups
    rows = ghost_tx.shape[1]
    ups, asks = peers * POOL_PAD, peers * ASK
    few, some = pl.ds(0, POOL), pl.ds(0, ASK)
    ones = averager()

    fetch = pltpu.make_async_copy(edges_hbm, edges, fetch_sems.at[0])
    fetch.start()
    cfetch = pltpu.make_async_copy(cedges_hbm, cedges, fetch_sems.at[1])
    cfetch.start()
    up_rx[...] = jnp.zeros_like(up_rx)
    down_rx[...] = jnp.zeros_like(down_rx)
    greet(("dom", "grp"))

    local = local_ref[...]
    picks = dot(pick_rows(column(ghost_ids[...]), nodes), local)
    for p in range(peers):
        ghost_tx[p] = picks[p * rows : (p + 1) * rows].astype(BF)
    parent = parents[...]
    owner, within = parent >> shift, parent & (own - 1)
    rank, theirs = ranked(owner, peers)
    away = owner != me
    place = jnp.where(away, own + owner * POOL_PAD + rank, within)
    excess = jnp.max(jnp.where(away & (rank >= POOL), 1, 0), axis=1, keepdims=True)
    note = listed(theirs, within, rank + lax.rem(me, 4) * POOL_PAD)
    for p in range(peers):
        note_tx[p, :, 0:128] = note[p : p + 1]
    chunk = csenders.shape[1]
    before = as_bf(iota((chunk, chunk), 0) < iota((chunk, chunk), 1))
    senders = csenders[...]
    owners, withins = senders >> shift, senders & (own - 1)
    theirs = [iota((peers, chunk), 0) == owners[k : k + 1] for k in range(groups)]
    counts = dot(jnp.concatenate([as_bf(t) for t in theirs], 0), before)
    past = jnp.zeros((peers, 1), F32)
    cslots, lists, lanes = [], [], []
    for k in range(groups):
        count = counts[k * peers : (k + 1) * peers] + past
        rank = jnp.sum(jnp.where(theirs[k], count, 0.0), axis=0, keepdims=True).astype(I32)
        past = past + jnp.sum(jnp.where(theirs[k], 1.0, 0.0), axis=1, keepdims=True)
        mine, place_ = lax.rem(rank, groups) == grp, rank // groups
        cslots.append(jnp.where(mine & (place_ < ASK), owners[k : k + 1] * ASK + place_, -1))
        lists.append(theirs[k] & mine)
        lanes.append(place_ + lax.rem(me, 4) * POOL_PAD)
    full = jnp.max(past, axis=0, keepdims=True) > float(groups * ASK)
    excess = jnp.maximum(excess, jnp.where(full, 1, 0))
    joined = lambda parts: jnp.concatenate(parts, 1)
    note = listed(joined(lists), joined([withins[k : k + 1] for k in range(groups)]), joined(lanes))
    for p in range(peers):
        note_tx[p, :, 128:256] = note[p : p + 1]
    flag_tx[...] = jnp.broadcast_to(excess, (1, 128))

    w_mean[0] = mean_of(out_w[0])
    w_mean[1] = mean_of(out_w[1])
    by_sender[:, :128] = dot(local, ein_ref[0, 256:384, :]).astype(BF)
    mine = dot(local, ein_ref[0, 128:256, :]).astype(BF)
    by_receiver[:, :128] = mine[:half]
    by_receiver[:, 128:] = mine[half:]
    total[...] = jnp.zeros_like(total)
    fetch.wait()

    def first_part(i, carry):
        at = pl.ds(pl.multiple_of(i * block, block), block)
        rcol = column(rcv_ref[i])
        upper = rcol >= half
        from_r = dot(pick_rows(jnp.where(upper, rcol - half, rcol), half), by_receiver[...])
        partial[at, :] = dot(edges[at, :], ein_ref[0, 0:128, :]) + jnp.where(upper, from_r[:, 128:], from_r[:, :128])
        return carry

    early = EARLY_BLOCKS
    lax.fori_loop(0, early, first_part, 0)
    all_here(("dom", "grp"))
    send("dom", lambda p: ghost_tx.at[p], lambda m: ghost_rx.at[m], sems.at[8])
    send("grp", lambda p: flag_tx, lambda m: flag_rx.at[m], sems.at[9])
    ghost_rx[me] = ghost_tx[me]
    flag_rx[grp] = flag_tx[...]
    lax.fori_loop(early, blocks, first_part, 0)
    cfetch.wait()
    gathered = jnp.zeros((asks, 256), F32)
    lane = iota((chunk, 128), 1)
    for k in range(groups):
        to = column(crecv_ref[k : k + 1])
        facts = jnp.where(lane == 0, to & 255, jnp.where(lane == 1, to >> 8, jnp.where(lane == 2, 1, 0)))
        data = jnp.concatenate([cedges[k * chunk : (k + 1) * chunk], facts.astype(F32).astype(BF)], 1)
        gathered += dot(pick_into(cslots[k], asks), data)
    cedge[...] = gathered[:, :128].astype(BF)
    to = gathered[:, 128:129] + 256.0 * gathered[:, 129:130] + (gathered[:, 130:131] - 1.0)
    cto[...] = jnp.broadcast_to(to, (asks, 128)).astype(I32)
    fsel[...] = pick_rows(column(place), own + ups)
    arrived("grp", flag_rx.at[pl.ds(0, friends)], sems.at[9])
    flag = flag_rx[0]
    for k in range(1, groups):
        flag = jnp.maximum(flag, flag_rx[k])
    for p in range(peers):
        note_tx[p, :, 256:384] = flag
    arrived("dom", ghost_rx.at[pl.ds(0, others)], sems.at[8])
    send("dom", lambda p: note_tx.at[p], lambda m: note_rx.at[m], sems.at[10])
    note_rx[me] = jnp.concatenate([jnp.zeros((1, 128), I32), note_tx[me, :, 128:384]], 1)

    ghosts = ghost_rx[...].astype(F32).reshape(nodes, 128).astype(BF)
    by_sender[:, 128:] = dot(ghosts, ein_ref[0, 256:384, :]).astype(BF)

    def second_part(i, carry):
        at = pl.ds(pl.multiple_of(i * block, block), block)
        receivers = rcv_ref[i]
        scol, rcol = column(snd_ref[i]), column(receivers)
        s_upper, r_upper = scol >= nodes, rcol >= half
        from_s = dot(pick_rows(jnp.where(s_upper, scol - nodes, scol), nodes), by_sender[...])
        x = partial[at, :] + jnp.where(s_upper, from_s[:, 128:], from_s[:, :128])
        new = edges[at, :].astype(F32) + second(x, w_mean[0], ones)
        sides = jnp.concatenate([jnp.where(r_upper, 0.0, new), jnp.where(r_upper, new, 0.0)], 1)
        slot = i * block + iota((1, block), 1)
        into = jnp.where(receivers >= half, receivers - half, receivers)
        into = jnp.where(slot < count_ref[...], into, -1)
        total[...] += dot(pick_into(into, half), sides.astype(BF))
        return carry

    lax.fori_loop(0, blocks, second_part, 0)
    agg = jnp.concatenate([total[:, :128], total[:, 128:]], 0).astype(BF)
    x = dot(local, nin_ref[0, 0:128, :]) + dot(agg, nin_ref[0, 128:256, :])
    mid = (local.astype(F32) + second(x, w_mean[1], ones)).astype(BF)

    up_tx[...] = dot(pick_into(place, ups, own), mid).astype(BF).reshape(up_tx.shape)
    send("dom", lambda p: up_tx.at[p, few], lambda m: up_rx.at[m, few], sems.at[0])
    mid_out[...] = mid

    arrived("dom", note_rx.at[pl.ds(0, others)], sems.at[10])
    flag = note_rx[0, :, 256:384]
    for p in range(1, peers):
        flag = jnp.maximum(flag, note_rx[p, :, 256:384])
    flag_out[...] = flag
    pool_rows = [sum(note_rx[p, :, 0:128] for p in range(k, k + 4)) - 1 for k in range(0, peers, 4)]
    ask_rows = [sum(note_rx[p, :, 128:256] for p in range(k, k + 4)) - 1 for k in range(0, peers, 4)]
    here = pick_into(place, own)
    there = pick_into(jnp.concatenate(pool_rows, 1), own)
    counts = lax.dot_general(jnp.full((8, nodes), 1.0, BF), here, NT, preferred_element_type=F32)
    counts += lax.dot_general(jnp.full((8, ups), 1.0, BF), there, NT, preferred_element_type=F32)
    count_tx[...] = counts[0:1]
    send("grp", lambda p: count_tx, lambda m: count_rx.at[m], sems.at[1])
    count_rx[grp] = count_tx[...]
    pooled = dot(here, mid)
    for k, row in enumerate(ask_rows):
        ask_sel[128 * k : 128 * (k + 1), :] = pick_rows(column(row), own)
    for k, row in enumerate(pool_rows):
        down_sel[128 * k : 128 * (k + 1), :] = pick_rows(column(row), own)
    to = cto[...]
    from_r = pick_rows(to, own)
    into = pick_into(jnp.concatenate([to[k : k + 128].T[0:1] for k in range(0, asks, 128)], 1), own)
    w_edge, w_node, w_back = mean_of(out_w[2]), mean_of(out_w[3]), mean_of(out_w[4])
    arrived("grp", count_rx.at[pl.ds(0, friends)], sems.at[1])
    children = count_rx[0]
    for k in range(1, groups):
        children = children + count_rx[k]
    diagonal = iota((piece, own), 1) == iota((piece, own), 0) + grp * piece
    children = jnp.sum(jnp.where(diagonal, children, 0.0), axis=1, keepdims=True)

    arrived("dom", up_rx.at[pl.ds(0, others), few], sems.at[0])
    pooled += dot(there, up_rx[...].reshape(ups, 128))
    part_tx[...] = pooled.astype(BF).reshape(part_tx.shape)
    send("grp", lambda p: part_tx.at[p], lambda m: part_rx.at[m], sems.at[2])
    part_rx[grp] = part_tx[grp]
    arrived("grp", part_rx.at[pl.ds(0, friends)], sems.at[2])
    mine = pl.ds(pl.multiple_of(grp * piece, piece), piece)
    sums = cnodes_ref[mine, :].astype(F32)
    for k in range(groups):
        sums = sums + part_rx[k].astype(F32)
    own_mid = (sums / (1.0 + children)).astype(BF)
    cmid[grp] = own_mid
    send("grp", lambda p: cmid.at[grp], lambda m: cmid.at[m], sems.at[3])
    arrived("grp", cmid.at[pl.ds(0, friends)], sems.at[3])

    coarse = cmid[...].reshape(own, 128)
    ask_tx[...] = dot(ask_sel[...], coarse).astype(BF).reshape(ask_tx.shape)
    send("dom", lambda p: ask_tx.at[p, some], lambda m: ask_rx.at[m], sems.at[4])
    ask_rx[me] = ask_tx[me, 0:ASK]
    edge = cedge[...]
    x = dot(edge, ein_ref[1, 0:128, :]) + dot(dot(from_r, coarse).astype(BF), ein_ref[1, 128:256, :])
    arrived("dom", ask_rx.at[pl.ds(0, others)], sems.at[4])
    x += dot(ask_rx[...].astype(F32).reshape(asks, 128).astype(BF), ein_ref[1, 256:384, :])
    new = edge.astype(F32) + second(x, w_edge, ones)
    cpart_tx[...] = dot(into, new.astype(BF)).astype(BF).reshape(cpart_tx.shape)
    send("grp", lambda p: cpart_tx.at[p], lambda m: cpart_rx.at[m], sems.at[5])
    cpart_rx[grp] = cpart_tx[grp]
    x = dot(own_mid, nin_ref[1, 0:128, :])
    arrived("grp", cpart_rx.at[pl.ds(0, friends)], sems.at[5])
    sums = cpart_rx[0].astype(F32)
    for k in range(1, groups):
        sums = sums + cpart_rx[k].astype(F32)
    x += dot(sums.astype(BF), nin_ref[1, 128:256, :])
    cout[grp] = (own_mid.astype(F32) + second(x, w_node, ones)).astype(BF)
    send("grp", lambda p: cout.at[grp], lambda m: cout.at[m], sems.at[6])
    arrived("grp", cout.at[pl.ds(0, friends)], sems.at[6])

    coarse = cout[...].reshape(own, 128)
    down_tx[...] = dot(down_sel[...], coarse).astype(BF).reshape(down_tx.shape)
    send("dom", lambda p: down_tx.at[p, few], lambda m: down_rx.at[m, few], sems.at[7])
    coarse_out[...] = coarse
    above = dot(fsel[:, 0:own], coarse)
    x = dot(mid, nin_ref[2, 0:128, :])
    arrived("dom", down_rx.at[pl.ds(0, others), few], sems.at[7])
    above += dot(fsel[:, own:], down_rx[...].reshape(ups, 128))
    x += dot(above.astype(BF), nin_ref[2, 128:256, :])
    fine_out[...] = (mid.astype(F32) + second(x, w_back, ones)).astype(BF)


def whole_step(
    count, edges, senders, receivers, local, ghost_send, parents, coarse_nodes, coarse_edges, coarse_senders,
    coarse_receivers, edge_in, node_in, mlp_out,
):
    peers, groups = lax.axis_size("dom"), lax.axis_size("grp")
    own, nodes, slots, rows = coarse_nodes.shape[0], local.shape[0], edges.shape[0], ghost_send.shape[1]
    nedges, piece = coarse_edges.shape[0], own // groups
    blocks = slots // BLOCK
    buffer = lambda *shape: pltpu.VMEM(shape, BF)
    pair = lambda *shape: [buffer(*shape), buffer(*shape)]
    anywhere = [pl.BlockSpec(memory_space=pl.ANY)]
    return pl.pallas_call(
        step_kernel,
        name="step",
        out_shape=[
            jax.ShapeDtypeStruct((nodes, 128), BF), jax.ShapeDtypeStruct((own, 128), BF),
            jax.ShapeDtypeStruct((nodes, 128), BF), jax.ShapeDtypeStruct((1, 128), I32),
        ],
        in_specs=vmem(1) + anywhere + vmem(7) + anywhere + vmem(4),
        out_specs=vmem(4),
        scratch_shapes=[
            buffer(slots, 128), pltpu.VMEM((slots, 128), F32), buffer(nodes, 256), buffer(nodes // 2, 256),
            pltpu.VMEM((nodes // 2, 256), F32), buffer(2, 128, 256), buffer(nedges, 128),
            *pair(peers, rows, 128),
            pltpu.VMEM((peers, 1, 384), I32), pltpu.VMEM((peers, 1, 384), I32),
            pltpu.VMEM((1, 128), I32), pltpu.VMEM((groups, 1, 128), I32),
            *pair(peers, POOL_PAD, 128),
            pltpu.VMEM((1, own), F32), pltpu.VMEM((groups, 1, own), F32),
            *pair(groups, piece, 128), buffer(groups, piece, 128),
            buffer(peers, POOL_PAD, 128), buffer(peers, ASK, 128),
            *pair(groups, piece, 128), buffer(groups, piece, 128),
            *pair(peers, POOL_PAD, 128),
            buffer(peers * POOL_PAD, own), buffer(peers * POOL_PAD, own),
            buffer(nodes, own + peers * POOL_PAD), buffer(peers * ASK, 128), pltpu.VMEM((peers * ASK, 128), I32),
            pltpu.SemaphoreType.DMA((2,)), pltpu.SemaphoreType.DMA((11, 2)),
        ],
        compiler_params=pltpu.CompilerParams(collective_id=0, has_side_effects=True),
    )(
        count, edges, senders.reshape(blocks, 1, BLOCK), receivers.reshape(blocks, 1, BLOCK), local,
        ghost_send.reshape(1, -1), parents.reshape(1, -1), coarse_senders.reshape(groups, -1),
        coarse_nodes, coarse_edges, coarse_receivers.reshape(groups, -1), edge_in, node_in, mlp_out,
    )


def layer_norm(values):
    centre = values - jnp.mean(values, -1, keepdims=True)
    spread = jnp.mean(centre * centre, -1, keepdims=True)
    return centre * lax.rsqrt(spread + 1e-05)


def perceptron(inputs, w_first, w_second):
    hidden = jax.nn.silu(jnp.dot(inputs, w_first, preferred_element_type=F32)).astype(BF)
    return layer_norm(jnp.dot(hidden, w_second, preferred_element_type=F32))


def summed(array, axis):
    return jnp.sum(lax.all_to_all(array, axis, 0, 0, tiled=True), axis=0)


def all_of(array, axis):
    peers = lax.axis_size(axis)
    copies = lax.all_to_all(jnp.broadcast_to(array[None], (peers, *array.shape)), axis, 0, 0, tiled=True)
    return copies.reshape(peers * array.shape[0], *array.shape[1:])


def dense_step(
    mid, parents, coarse_nodes, coarse_edges, coarse_senders, coarse_receivers, edge_in, node_in, mlp_out
):
    peers, groups = lax.axis_size("dom"), lax.axis_size("grp")
    own = coarse_nodes.shape[0]
    piece = own // groups
    wide = jnp.concatenate([mid.astype(F32), jnp.ones(mid.shape, F32)], -1)
    sums = jax.ops.segment_sum(wide, parents, num_segments=own * peers)
    sums = jnp.moveaxis(sums.reshape(peers, groups, piece, 256), 1, 0)
    sums = all_of(summed(summed(sums, "grp"), "dom"), "grp")
    coarse_mid = ((coarse_nodes.astype(F32) + sums[:, :128]) / (1.0 + sums[:, 128:])).astype(BF)
    table = all_of(coarse_mid, "dom")
    inputs = jnp.concatenate([coarse_edges, coarse_mid[coarse_receivers], table[coarse_senders]], -1)
    new = coarse_edges.astype(F32) + perceptron(inputs, edge_in[1], mlp_out[2])
    agg = jax.ops.segment_sum(new, coarse_receivers, num_segments=own).astype(BF)
    out = perceptron(jnp.concatenate([coarse_mid, agg], -1), node_in[1], mlp_out[3])
    coarse_out = (coarse_mid.astype(F32) + out).astype(BF)
    above = all_of(coarse_out, "dom")[parents]
    back = perceptron(jnp.concatenate([mid, above], -1), node_in[2], mlp_out[4])
    return (mid.astype(F32) + back).astype(BF), coarse_out


def per_device(
    fine_nodes, fine_edges, fine_senders, fine_receivers, edge_count, ghost_send, fine_parent, coarse_nodes,
    coarse_edges, coarse_senders, coarse_receivers, edge_in, node_in, mlp_out,
):
    parents = fine_parent[0]
    fine_out, coarse_out, mid, flag = whole_step(
        edge_count, fine_edges[0], fine_senders[0], fine_receivers[0], fine_nodes[0], ghost_send[0], parents,
        coarse_nodes, coarse_edges, coarse_senders, coarse_receivers, edge_in, node_in, mlp_out,
    )

    def again():
        return dense_step(
            mid, parents, coarse_nodes, coarse_edges, coarse_senders, coarse_receivers, edge_in, node_in, mlp_out
        )

    fine_out, coarse_out = lax.cond(flag[0, 0] > 0, again, lambda: (fine_out, coarse_out))
    return (fine_out[None], coarse_out)


def solution(mesh):
    fine, coarse = P("grp", "dom"), P("dom")
    in_specs = (fine,) * 7 + (coarse,) * 4 + (P(),) * 3
    return jax.shard_map(
        per_device, mesh=mesh, in_specs=in_specs, out_specs=(fine, coarse), check_vma=False
    )
```
